32 devices in a mesh: fsdp: 8 (over z, y), ep: 4 (over x, core).
Axes of the slice: x: 2, y: 2, z: 4, core: 2. Of those that a mesh axis runs over, the one named last changes fastest.
Arguments:
- tokens: bfloat16 [4096, 3072], P(('fsdp', 'ep')), may hold values from -6 to 6
- expert_ids: int32 [4096, 2], P(('fsdp', 'ep')), may hold values from 0 to 3, all different within a row; in each aligned block of 128 rows (0 to 127, 128 to 255, ...) at most 128 rows name the same one
- gates: float32 [4096, 2], P(('fsdp', 'ep')), may hold values from 0.2 to 1
- up_weight: bfloat16 [4, 3072, 768], P('ep', 'fsdp'), may hold values from -0.109375 to 0.109375
- down_weight: bfloat16 [4, 768, 3072], P('ep', 'fsdp'), may hold values from -0.21875 to 0.21875
- cotangent: bfloat16 [4096, 3072], P(('fsdp', 'ep')), may hold values from -6 to 6
Outputs:
- mixed: bfloat16 [4096, 3072], P(('fsdp', 'ep'))
- token_grad: bfloat16 [4096, 3072], P(('fsdp', 'ep'))
- up_grad: bfloat16 [4, 3072, 768], P('ep', 'fsdp')
- down_grad: bfloat16 [4, 768, 3072], P('ep', 'fsdp')
The draws below stay inside these ranges and needn't reach their ends.
Inputs may be any that keep to these rules, and one draw needn't show every extreme that they name: `expert_ids`: each token names two different experts. Among the tokens of one device (aligned blocks of 128 tokens) no expert is named more than 128 times, and in some block one expert is named exactly 128 times.
All inputs are finite; a program needn't handle non-finite values.
Results may differ from the reference program's by a relative error of at most 0.012.
Values may be sent and summed in bfloat16 or wider, within the bound.
A program may use at most 128 MiB of HBM per device.

```python
import math
import jax
import jax.numpy as jnp
import numpy as np
from jax import lax

D = 3072
FF = 768
TOK_DEV = 128
CAP = 128
EXPERTS = 4
TOKENS = 4096
N_FSDP = 8
N_EP = 4


def levels(stream_key, extent, split, least, top_value):
    loudness, own = 1.0, jax.random.fold_in(stream_key, 6)
    for dim, parts in split:
        draws = jnp.exp(jax.random.uniform(jax.random.fold_in(own, dim), (parts,), jnp.float32, least / len(split), top_value / len(split)))
        loudness = loudness * jnp.repeat(draws, extent[dim] // parts).reshape([-1 if axis == dim else 1 for axis in range(len(extent))])
    return loudness


def assign_block(rng, own, number, rows, number_of, top, reach, skew):
    ranking = jax.random.permutation(rng, number_of)
    packed, usual = shares(number_of, rows * top, reach, skew, True), shares(number_of, rows * top, reach, skew, False)
    places = jnp.arange(number_of)

    def named(tallies, turn):
        used = int((tallies > 0).sum())
        fixed = max(1, used // 4)
        moved = fixed + (places - fixed + turn * (used - fixed)) % max(1, number_of - fixed)
        return jnp.zeros((number_of,), jnp.int32).at[ranking[jnp.where(places < fixed, places, moved)]].set(jnp.asarray(tallies, jnp.int32))

    tallies = jnp.where(number % 4 == 0, named(packed, number // 4), named(usual, number - number // 4 - 1))
    mixed = jax.random.permutation(jax.random.fold_in(own, 3), number_of)
    donor, taker = mixed[0:number_of // 2 * 2:2], mixed[1:number_of // 2 * 2:2]
    slack = jnp.minimum(tallies[donor] - 1, reach - tallies[taker]) // 2
    slack = jnp.where((donor == ranking[0]) | (taker == ranking[0]) | (tallies[taker] == 0), 0, jnp.maximum(slack, 0))
    moved = jax.random.randint(jax.random.fold_in(own, 4), (number_of // 2,), 0, 1 << 20) % (slack + 1)
    tallies = tallies.at[donor].add(-moved).at[taker].add(moved)
    items = jnp.searchsorted(jnp.cumsum(tallies), jnp.arange(rows * top), side="right").astype(jnp.int32)
    grid = items.reshape(top, rows).T
    grid = grid[jax.random.permutation(jax.random.fold_in(own, 1), rows)]
    turn = jax.random.randint(jax.random.fold_in(own, 2), (rows, 1), 0, top)
    return jnp.take_along_axis(grid, (jnp.arange(top)[None, :] + turn) % top, axis=1)


def shares(number_of, total, most, lean, full):
    loads = [(1 << 20) // math.isqrt(grade ** lean) + 1 for grade in range(1, number_of + 1)]
    largest = most if full else min(most, max(-(-total // number_of), total * loads[0] // sum(loads)))
    least = 1 if total - largest >= number_of - 1 else 0
    given, spare = [largest] + [least] * (number_of - 1), total - largest - least * (number_of - 1)
    while spare > 0:
        free = [i for i in range(1, number_of) if given[i] < largest] or [i for i in range(1, number_of) if given[i] < most]
        whole, remaining = sum([loads[i] for i in free]), spare
        for i in free:
            more = min(most - given[i], max(1, remaining * loads[i] // whole), spare)
            given[i] = given[i] + more
            spare = spare - more
    return np.array(given)


def centred(key, extent, scale, most, split=(), held_as=jnp.bfloat16):
    loudness = levels(key, extent, split, -0.22, 0.18) if split else 1.0
    values = jax.random.normal(key, extent, jnp.float32) * scale * loudness
    return jnp.minimum(jnp.maximum(values, -most), most).astype(held_as)


def setup_inputs(seed: int = 0) -> dict:
    splits = jax.random.split(jax.random.key(seed), 7)
    tokens = centred(splits[0], (TOKENS, D), 1.0, 6.0, ((0, 32),))
    expert_ids_keys = jax.random.split(jax.random.fold_in(splits[1], 1), TOKENS // TOK_DEV)
    expert_ids_turns = jax.random.permutation(jax.random.fold_in(splits[1], 3), TOKENS // TOK_DEV)
    expert_ids = jax.vmap(lambda own, number: assign_block(jax.random.fold_in(splits[1], 2), own, number, TOK_DEV, EXPERTS, 2, CAP, 2))(expert_ids_keys, expert_ids_turns).reshape((TOKENS, 2))
    gates = jnp.clip(0.2 + 0.8 * jax.random.uniform(splits[2], (TOKENS, 2), jnp.float32) ** levels(splits[2], (TOKENS, 2), ((0, 32),), -0.2, 0.2), 0.2, 1.0)
    up_weight = centred(splits[3], (EXPERTS, D, FF), D ** -0.5, 0.109375, ((0, 4), (1, 8)))
    down_weight = centred(splits[4], (EXPERTS, FF, D), FF ** -0.5, 0.21875, ((0, 4), (1, 8)))
    cotangent = centred(splits[5], (TOKENS, D), 1.0, 6.0, ((0, 32),))
    return dict(tokens=tokens, expert_ids=expert_ids, gates=gates, up_weight=up_weight, down_weight=down_weight, cotangent=cotangent)


def gelu_parts(pre):
    root = 0.7978845608028654
    inner = root * (pre + 0.044715 * pre * pre * pre)
    tanh_val = jnp.tanh(inner)
    value = 0.5 * pre * (1.0 + tanh_val)
    slope = 0.5 * (1.0 + tanh_val) + 0.5 * pre * (1.0 - tanh_val * tanh_val) * root * (1.0 + 3.0 * 0.044715 * pre * pre)
    return value, slope


def reference(tokens, expert_ids, gates, up_weight, down_weight, cotangent):
    width = tokens.shape[1]
    group = N_EP * TOK_DEV
    limit = N_EP * CAP
    flat_ids = expert_ids.reshape(-1)
    flat_gates = gates.reshape(-1)
    f32 = jnp.float32
    bf16 = jnp.bfloat16

    def per_expert(items):
        expert, up_mat, down_mat = items

        def per_group(index):
            chosen = lax.dynamic_slice_in_dim(flat_ids, index * 2 * group, 2 * group)
            hit = chosen == expert
            picks = jnp.nonzero(hit, size=limit, fill_value=0)[0].astype(jnp.int32)
            live = jnp.arange(limit, dtype=jnp.int32) < jnp.sum(hit.astype(jnp.int32))
            assign = (index * 2 * group + picks).astype(jnp.int32)
            rows = jnp.where(live[:, None], tokens[assign // 2], jnp.zeros((), bf16))
            pre = jnp.dot(rows, up_mat, preferred_element_type=f32)
            value, slope = gelu_parts(pre)
            hidden = value.astype(bf16)
            expert_out = jnp.dot(hidden, down_mat, preferred_element_type=f32).astype(bf16)
            scaled = (cotangent[assign // 2].astype(f32) * flat_gates[assign][:, None]).astype(bf16)
            grad_rows = jnp.where(live[:, None], scaled, jnp.zeros((), bf16))
            d_hidden = jnp.dot(grad_rows, down_mat.T, preferred_element_type=f32)
            d_pre = (d_hidden * slope).astype(bf16)
            back_rows = jnp.dot(d_pre, up_mat.T, preferred_element_type=f32).astype(bf16)
            up_part = jnp.dot(rows.T, d_pre, preferred_element_type=f32).astype(bf16)
            down_part = jnp.dot(hidden.T, grad_rows, preferred_element_type=f32).astype(bf16)
            place = jnp.where(live, assign, 2 * TOKENS)
            return expert_out, back_rows, place, up_part, down_part

        outs, backs, places, up_parts, down_parts = lax.map(per_group, jnp.arange(N_FSDP, dtype=jnp.int32))
        up_total = jnp.sum(up_parts.astype(f32), axis=0).astype(bf16)
        down_total = jnp.sum(down_parts.astype(f32), axis=0).astype(bf16)
        return outs, backs, places, up_total, down_total

    outs, backs, places, up_grad, down_grad = lax.map(
        per_expert, (jnp.arange(N_EP, dtype=jnp.int32), up_weight, down_weight))
    flat_places = places.reshape(-1)
    assigned = jnp.zeros((2 * TOKENS, width), f32).at[flat_places].add(
        outs.reshape(-1, width).astype(f32), mode="drop")
    returned = jnp.zeros((2 * TOKENS, width), f32).at[flat_places].add(
        backs.reshape(-1, width).astype(f32), mode="drop")
    mixed = jnp.sum(assigned.reshape(TOKENS, 2, width) * gates[:, :, None], axis=1).astype(bf16)
    token_grad = jnp.sum(returned.reshape(TOKENS, 2, width), axis=1).astype(bf16)
    return mixed, token_grad, up_grad, down_grad
```

```python
import jax
import jax.numpy as jnp
from jax import lax
from jax.sharding import PartitionSpec as P


def gelu_parts(pre):
    root = 0.7978845608028654
    inner = root * (pre + 0.044715 * pre * pre * pre)
    tanh_val = jnp.tanh(inner)
    value = 0.5 * pre * (1.0 + tanh_val)
    slope = 0.5 * (1.0 + tanh_val) + 0.5 * pre * (1.0 - tanh_val * tanh_val) * root * (
        1.0 + 3.0 * 0.044715 * pre * pre
    )
    return (value, slope)


def contract_last(left, right):
    return lax.dot_general(
        left, right, (((1,), (1,)), ((), ())), preferred_element_type=jnp.float32
    )


def contract_first(left, right):
    return lax.dot_general(
        left, right, (((0,), (0,)), ((), ())), preferred_element_type=jnp.float32
    )


def body(tokens, expert_ids, gates, up_weight, down_weight, cotangent):
    n_ep = lax.axis_size("ep")
    f32 = jnp.float32
    bf16 = jnp.bfloat16
    chosen = expert_ids[:, :, None] == jnp.arange(n_ep, dtype=jnp.int32)[None, None, :]
    dense_gates = jnp.sum(jnp.where(chosen, gates[:, :, None], 0.0), axis=1)
    all_gates = lax.all_gather(dense_gates, "ep", axis=0, tiled=True)
    mine = lax.axis_index("ep") == jnp.arange(n_ep, dtype=jnp.int32)
    gate = jnp.sum(jnp.where(mine[None, :], all_gates, 0.0), axis=1, keepdims=True)
    rows = lax.all_gather(tokens, "ep", axis=0, tiled=True)
    up = lax.all_gather(up_weight, "fsdp", axis=1, tiled=True)[0]
    cot = lax.all_gather(cotangent, "ep", axis=0, tiled=True)
    down = lax.all_gather(down_weight, "fsdp", axis=1, tiled=True)[0]
    grad_rows = (cot.astype(f32) * gate).astype(bf16)
    pre = jnp.dot(rows, up, preferred_element_type=f32)
    value, slope = gelu_parts(pre)
    hidden = value.astype(bf16)
    down_grad = lax.psum_scatter(
        contract_first(hidden, grad_rows).astype(bf16), "fsdp", scatter_dimension=0, tiled=True
    )
    d_hidden = contract_last(grad_rows, down)
    d_pre = (d_hidden * slope).astype(bf16)
    up_grad = lax.psum_scatter(
        contract_first(rows, d_pre).astype(bf16), "fsdp", scatter_dimension=0, tiled=True
    )
    result = jnp.dot(hidden, down, preferred_element_type=f32)
    mixed = lax.psum_scatter((result * gate).astype(bf16), "ep", scatter_dimension=0, tiled=True)
    back = contract_last(d_pre, up).astype(bf16)
    token_grad = lax.psum_scatter(back, "ep", scatter_dimension=0, tiled=True)
    return (mixed, token_grad, up_grad[None], down_grad[None])


def solution(mesh):
    placed = (
        P(("fsdp", "ep"), None),
        P(("fsdp", "ep"), None),
        P(("fsdp", "ep"), None),
        P("ep", "fsdp", None),
        P("ep", "fsdp", None),
        P(("fsdp", "ep"), None),
    )
    return jax.shard_map(
        body,
        mesh=mesh,
        in_specs=placed,
        out_specs=(
            P(("fsdp", "ep"), None),
            P(("fsdp", "ep"), None),
            P("ep", "fsdp", None),
            P("ep", "fsdp", None),
        ),
        check_vma=False,
    )
```

```python
import functools

import jax
import jax.numpy as jnp
from jax import lax
from jax.experimental import pallas as pl
from jax.experimental.pallas import tpu as pltpu
from jax.sharding import PartitionSpec as P

F32 = jnp.float32
BF16 = jnp.bfloat16
MESH = pl.DeviceIdType.MESH
LANES = 128


def gelu_parts(pre):
    root = 0.7978845608028654
    inner = root * (pre + 0.044715 * pre * pre * pre)
    tanh_val = jnp.tanh(inner)
    value = 0.5 * pre * (1.0 + tanh_val)
    slope = 0.5 * (1.0 + tanh_val) + 0.5 * pre * (1.0 - tanh_val * tanh_val) * root * (
        1.0 + 3.0 * 0.044715 * pre * pre
    )
    return (value, slope)


def dot(left, right, dims):
    return lax.dot_general(left, right, (dims, ((), ())), preferred_element_type=F32)


NN = ((1,), (0,))
NT = ((1,), (1,))
TN = ((0,), (0,))


def tiles(count, size):
    def run(fn):
        @pl.loop(0, count // size)
        def _(i):
            fn(pl.ds(pl.multiple_of(i * size, size), size))

    return run


def kernel(
    nz, ny, nx,
    tok_in, cot_in, gate_in, up_in, down_in,
    mixed_out, tg_out, ug_out, dg_out,
    up, down, tok, cot, gate, slope, hidden, dpre, upart, dpart,
    ry_u, ry_d, rz_u, rz_d, rc_m, rc_t, rx_m, rx_t,
    local_sem, wz_s, wz_r, wy_s, wy_r, tx_s, tx_r, tc_s, tc_r, g_s, g_r,
    ry_s, ry_r, rz_s, rz_r, rc_s, rc_r, rx_s, rx_r,
):
    ne = 2 * nx
    f = lax.axis_index("fsdp")
    e = lax.axis_index("ep")
    z, y = lax.div(f, ny), lax.rem(f, ny)
    x, c = lax.div(e, 2), lax.rem(e, 2)
    T = tok_in.shape[0]
    D = tok_in.shape[1]
    R = ne * T
    FF = up.shape[1]

    def zp(k):
        return lax.rem(z + k + nz, nz)

    def yp(j):
        return lax.rem(y + j + ny, ny)

    def xp(k):
        return lax.rem(x + k + nx, nx)

    def fdev(zz, yy):
        return {"fsdp": zz * ny + yy}

    def edev(xx, cc):
        return {"ep": xx * 2 + cc}

    def rows(ref, index, size):
        return ref.at[pl.ds(pl.multiple_of(index * size, size), size)]

    def remote(src, dst, ss, rs, dev):
        return pltpu.make_async_remote_copy(
            src_ref=src, dst_ref=dst, send_sem=ss, recv_sem=rs,
            device_id=dev, device_id_type=MESH,
        )

    sends = []

    def send(src, dst, ss, rs, dev):
        copy = remote(src, dst, ss, rs, dev)
        copy.start()
        sends.append(copy)
        return copy

    barrier = pltpu.get_barrier_semaphore()
    peers = [fdev(zp(k), y) for k in range(1, nz)]
    peers += [fdev(z, yp(j)) for j in range(1, ny)]
    peers += [{"ep": lax.rem(e + i, ne)} for i in range(1, ne)]
    for dev in peers:
        pl.semaphore_signal(barrier, inc=1, device_id=dev, device_id_type=MESH)
    locals_ = []
    for i, (src, dst) in enumerate((
        (up_in.at[0], rows(up, f, up_in.shape[1])),
        (down_in.at[0], rows(down, f, down_in.shape[1])),
        (tok_in, rows(tok, e, T)),
        (cot_in, rows(cot, e, T)),
    )):
        copy = pltpu.make_async_copy(src, dst, local_sem.at[i])
        copy.start()
        locals_.append(copy)
    rows(gate, e, T)[...] = gate_in[e]
    pl.semaphore_wait(barrier, len(peers))

    weights = ((up_in, up), (down_in, down))
    zorder = [1, nz - 1] + list(range(2, nz - 1))

    def weight_start(w):
        src, full = weights[w]
        size = src.shape[1]
        for k in zorder:
            send(src.at[0], rows(full, f, size), wz_s.at[w, k - 1], wz_r.at[w, k - 1],
                 fdev(zp(k), y))
        for j in range(1, ny):
            send(src.at[0], rows(full, f, size), wy_s.at[w, 0, j - 1], wy_r.at[w, 0, j - 1],
                 fdev(z, yp(j)))

    def weight_forward(w):
        src, full = weights[w]
        size = src.shape[1]
        for k in zorder:
            block = rows(full, zp(-k) * ny + y, size)
            remote(block, block, wz_s.at[w, k - 1], wz_r.at[w, k - 1],
                   fdev(zp(k), y)).wait_recv()
            for j in range(1, ny):
                send(block, block, wy_s.at[w, k, j - 1], wy_r.at[w, k, j - 1], fdev(z, yp(j)))

    def weight_wait(w):
        src, full = weights[w]
        size = src.shape[1]
        locals_[w].wait()
        for k in [0] + zorder:
            for j in range(1, ny):
                block = rows(full, zp(-k) * ny + yp(-j), size)
                remote(block, block, wy_s.at[w, k, j - 1], wy_r.at[w, k, j - 1],
                       fdev(z, yp(j))).wait_recv()

    acts = ((tok_in, tok), (cot_in, cot))

    def act_start(w):
        src, full = acts[w]
        for k in range(1, nx):
            send(src, rows(full, e, T), tx_s.at[w, k - 1], tx_r.at[w, k - 1], edev(xp(k), c))
        send(src, rows(full, e, T), tc_s.at[w, 0], tc_r.at[w, 0], edev(x, 1 - c))

    def act_forward(w):
        src, full = acts[w]
        started = []
        for k in range(1, nx):
            block = rows(full, xp(-k) * 2 + c, T)
            remote(block, block, tx_s.at[w, k - 1], tx_r.at[w, k - 1],
                   edev(xp(k), c)).wait_recv()
            copy = remote(block, block, tc_s.at[w, k], tc_r.at[w, k], edev(x, 1 - c))
            copy.start()
            started.append(copy)
        return started

    def act_wait(w):
        src, full = acts[w]
        locals_[2 + w].wait()
        for k in range(nx):
            block = rows(full, xp(-k) * 2 + 1 - c, T)
            remote(block, block, tc_s.at[w, k], tc_r.at[w, k], edev(x, 1 - c)).wait_recv()

    weight_start(0)
    act_start(0)
    for i in range(1, ne):
        other = lax.rem(e + i, ne)
        send(gate_in.at[other], rows(gate, e, T), g_s.at[i - 1], g_r.at[i - 1], {"ep": other})
    act_start(1)
    tok_forwards = act_forward(0)
    weight_forward(0)
    weight_start(1)
    cot_forwards = act_forward(1)

    act_wait(1)
    for copy in cot_forwards:
        copy.wait_send()
    for i in range(1, ne):
        block = rows(gate, lax.rem(e - i + ne, ne), T)
        remote(block, block, g_s.at[i - 1], g_r.at[i - 1], {"ep": lax.rem(e + i, ne)}).wait_recv()

    @tiles(R, 16)
    def _(r):
        cot[r, :] = (cot[r, :].astype(F32) * gate[r, 0:1]).astype(BF16)

    act_wait(0)
    weight_wait(0)

    @tiles(FF, 256)
    def _(n):
        slope[:, n] = dot(tok[...], up[:, n], NN)

    @tiles(R, 16)
    def _(r):
        value, grad = gelu_parts(slope[r, :])
        hidden[r, :] = value.astype(BF16)
        slope[r, :] = grad

    @tiles(D, 512)
    def _(n):
        dpart[:, n] = dot(hidden[...], cot[:, n], TN).astype(BF16)

    parts = ((upart, ry_u, rz_u, ug_out), (dpart, ry_d, rz_d, dg_out))

    def part_start(w):
        part, ry, rz, out = parts[w]
        size = out.shape[1]
        for k in zorder + [0]:
            for j in range(1, ny):
                send(rows(part, zp(k) * ny + yp(j), size), ry.at[(j - 1) * nz + k],
                     ry_s.at[w, k, j - 1], ry_r.at[w, k, j - 1], fdev(z, yp(j)))

    def part_pair(w):
        part, ry, rz, out = parts[w]
        size = out.shape[1]
        for k in zorder + [0]:
            index = zp(k) * ny + y
            for j in range(1, ny):
                slot = ry.at[(j - 1) * nz + k]
                remote(slot, slot, ry_s.at[w, k, j - 1], ry_r.at[w, k, j - 1],
                       fdev(z, yp(j))).wait_recv()

            @tiles(size, 16)
            def _(r):
                at = pl.ds(pl.multiple_of(index * size + r.start, 16), 16)
                total = part[at, :].astype(F32)
                for j in range(1, ny):
                    total += ry[(j - 1) * nz + k, r, :].astype(F32)
                part[at, :] = total.astype(BF16)

            if k:
                send(rows(part, index, size), rz.at[k - 1], rz_s.at[w, k - 1],
                     rz_r.at[w, k - 1], fdev(zp(k), y))

    def part_end(w):
        part, ry, rz, out = parts[w]
        size = out.shape[1]
        for k in zorder:
            slot = rz.at[k - 1]
            remote(slot, slot, rz_s.at[w, k - 1], rz_r.at[w, k - 1], fdev(zp(k), y)).wait_recv()

        @tiles(size, 16)
        def _(r):
            at = pl.ds(pl.multiple_of(f * size + r.start, 16), 16)
            total = part[at, :].astype(F32)
            for k in zorder:
                total += rz[k - 1, r, :].astype(F32)
            out[0, r, :] = total.astype(BF16)

    backs = ((cot, rc_m, rx_m, mixed_out), (tok, rc_t, rx_t, tg_out))

    def back_start(w):
        full, rc, rx, out = backs[w]
        for k in range(nx):
            k = (k + 1) % nx
            send(rows(full, xp(k) * 2 + 1 - c, T), rc.at[k], rc_s.at[w, k], rc_r.at[w, k],
                 edev(x, 1 - c))

    def back_pair(w):
        full, rc, rx, out = backs[w]
        for k in range(nx):
            k = (k + 1) % nx
            index = xp(k) * 2 + c
            slot = rc.at[k]
            remote(slot, slot, rc_s.at[w, k], rc_r.at[w, k], edev(x, 1 - c)).wait_recv()

            @tiles(T, 16)
            def _(r):
                at = pl.ds(pl.multiple_of(index * T + r.start, 16), 16)
                full[at, :] = (full[at, :].astype(F32) + rc[k, r, :].astype(F32)).astype(BF16)

            if k:
                send(rows(full, index, T), rx.at[k - 1], rx_s.at[w, k - 1], rx_r.at[w, k - 1],
                     edev(xp(k), c))

    def back_end(w):
        full, rc, rx, out = backs[w]
        for k in range(1, nx):
            slot = rx.at[k - 1]
            remote(slot, slot, rx_s.at[w, k - 1], rx_r.at[w, k - 1], edev(xp(k), c)).wait_recv()

        @tiles(T, 16)
        def _(r):
            at = pl.ds(pl.multiple_of(e * T + r.start, 16), 16)
            total = full[at, :].astype(F32)
            for k in range(1, nx):
                total += rx[k - 1, r, :].astype(F32)
            out[r, :] = total.astype(BF16)

    part_start(1)
    weight_forward(1)
    weight_wait(1)

    @tiles(FF, 256)
    def _(n):
        dpre[:, n] = (dot(cot[...], down[n, :], NT) * slope[:, n]).astype(BF16)

    @tiles(D, 384)
    def _(n):
        upart[n, :] = dot(tok[:, n], dpre[...], TN).astype(BF16)

    part_start(0)

    @tiles(D, 512)
    def _(n):
        cot[:, n] = (dot(hidden[...], down[:, n], NN) * gate[:, 0:1]).astype(BF16)

    back_start(0)
    for copy in tok_forwards:
        copy.wait_send()

    @tiles(D, 512)
    def _(n):
        tok[:, n] = dot(dpre[...], up[n, :], NT).astype(BF16)

    back_start(1)
    part_pair(1)
    back_pair(0)
    back_pair(1)
    part_pair(0)
    part_end(1)
    back_end(0)
    back_end(1)
    part_end(0)
    for copy in sends:
        copy.wait_send()


def body(tokens, expert_ids, gates, up_weight, down_weight, cotangent):
    nf, ne = lax.axis_size("fsdp"), lax.axis_size("ep")
    nz = 4
    ny, nx = nf // nz, ne // 2
    T, D = tokens.shape
    R = ne * T
    su, FF = up_weight.shape[1:]
    sd = down_weight.shape[1]
    chosen = expert_ids[None] == jnp.arange(ne, dtype=jnp.int32)[:, None, None]
    dense = jnp.sum(jnp.where(chosen, gates[None], 0.0), axis=2)
    gcols = jnp.broadcast_to(dense[:, :, None], (ne, T, LANES))
    anyspace = pl.BlockSpec(memory_space=pl.ANY)
    vmem = pl.BlockSpec(memory_space=pltpu.VMEM)
    sem = pltpu.SemaphoreType.DMA
    V = pltpu.VMEM
    scratch = [
        V((D, FF), BF16), V((FF, D), BF16), V((R, D), BF16), V((R, D), BF16),
        V((R, LANES), F32), V((R, FF), F32), V((R, FF), BF16), V((R, FF), BF16),
        V((D, FF), BF16), V((FF, D), BF16),
        V(((ny - 1) * nz, su, FF), BF16), V(((ny - 1) * nz, sd, D), BF16),
        V((nz - 1, su, FF), BF16), V((nz - 1, sd, D), BF16),
        V((nx, T, D), BF16), V((nx, T, D), BF16),
        V((nx - 1, T, D), BF16), V((nx - 1, T, D), BF16),
        sem((4,)),
        sem((2, nz - 1)), sem((2, nz - 1)),
        sem((2, nz, ny - 1)), sem((2, nz, ny - 1)),
        sem((2, nx - 1)), sem((2, nx - 1)),
        sem((2, nx)), sem((2, nx)),
        sem((ne - 1,)), sem((ne - 1,)),
        sem((2, nz, ny - 1)), sem((2, nz, ny - 1)),
        sem((2, nz - 1)), sem((2, nz - 1)),
        sem((2, nx)), sem((2, nx)),
        sem((2, nx - 1)), sem((2, nx - 1)),
    ]
    return pl.pallas_call(
        functools.partial(kernel, nz, ny, nx),
        out_shape=(
            jax.ShapeDtypeStruct((T, D), BF16),
            jax.ShapeDtypeStruct((T, D), BF16),
            jax.ShapeDtypeStruct((1, su, FF), BF16),
            jax.ShapeDtypeStruct((1, sd, D), BF16),
        ),
        in_specs=[anyspace, anyspace, vmem, anyspace, anyspace],
        out_specs=(vmem, vmem, vmem, vmem),
        scratch_shapes=scratch,
        compiler_params=pltpu.CompilerParams(
            collective_id=0, has_side_effects=True, vmem_limit_bytes=63 * 1024 * 1024
        ),
    )(tokens, cotangent, gcols, up_weight, down_weight)


def solution(mesh):
    placed = (
        P(("fsdp", "ep"), None),
        P(("fsdp", "ep"), None),
        P(("fsdp", "ep"), None),
        P("ep", "fsdp", None),
        P("ep", "fsdp", None),
        P(("fsdp", "ep"), None),
    )
    return jax.shard_map(
        body,
        mesh=mesh,
        in_specs=placed,
        out_specs=(
            P(("fsdp", "ep"), None),
            P(("fsdp", "ep"), None),
            P("ep", "fsdp", None),
            P("ep", "fsdp", None),
        ),
        check_vma=False,
    )
```

```python
import functools

import jax
import jax.numpy as jnp
from jax import lax
from jax.experimental import pallas as pl
from jax.experimental.pallas import tpu as pltpu
from jax.sharding import PartitionSpec as P

F32 = jnp.float32
BF16 = jnp.bfloat16
MESH = pl.DeviceIdType.MESH
LANES = 128


def gelu_parts(pre):
    root = 0.7978845608028654
    inner = root * (pre + 0.044715 * pre * pre * pre)
    tanh_val = jnp.tanh(inner)
    value = 0.5 * pre * (1.0 + tanh_val)
    slope = 0.5 * (1.0 + tanh_val) + 0.5 * pre * (1.0 - tanh_val * tanh_val) * root * (
        1.0 + 3.0 * 0.044715 * pre * pre
    )
    return (value, slope)


def dot(left, right, dims):
    return lax.dot_general(left, right, (dims, ((), ())), preferred_element_type=F32)


NN = ((1,), (0,))
NT = ((1,), (1,))
TN = ((0,), (0,))


def tail_rows(size):
    return max(16, size // 6 // 16 * 16)


def tiles(count, size):
    def run(fn):
        @pl.loop(0, count // size)
        def _(i):
            fn(pl.ds(pl.multiple_of(i * size, size), size))

    return run


def kernel(
    nz, ny, nx,
    tok_in, cot_in, gate_in, up_in, down_in,
    mixed_out, tg_out, ug_out, dg_out,
    up, down, tok, cot, gate, slope, hidden, dpre, upart, dpart,
    ry_u, ry_d, rz_u, rz_d, rt_u, rt_d, ft_u, ft_d, rc_m, rc_t, rx_m, rx_t,
    local_sem, wz_s, wz_r, wt_s, wt_r, wo_s, wo_r, wy_s, wy_r,
    tx_s, tx_r, tc_s, tc_r, g_s, g_r,
    ry_s, ry_r, rz_s, rz_r, rt_s, rt_r, ft_s, ft_r, rc_s, rc_r, rx_s, rx_r,
):
    ne = 2 * nx
    f = lax.axis_index("fsdp")
    e = lax.axis_index("ep")
    z, y = lax.div(f, ny), lax.rem(f, ny)
    x, c = lax.div(e, 2), lax.rem(e, 2)
    T = tok_in.shape[0]
    D = tok_in.shape[1]
    R = ne * T
    FF = up.shape[1]

    def zp(k):
        return lax.rem(z + k + nz, nz)

    def inside(zz):
        return (zz >= 0) & (zz < nz)

    def yp(j):
        return lax.rem(y + j + ny, ny)

    def xp(k):
        return lax.rem(x + k + nx, nx)

    def fdev(zz, yy):
        return {"fsdp": zz * ny + yy}

    def edev(xx, cc):
        return {"ep": xx * 2 + cc}

    def rows(ref, index, size):
        return ref.at[pl.ds(pl.multiple_of(index * size, size), size)]

    def remote(src, dst, ss, rs, dev):
        return pltpu.make_async_remote_copy(
            src_ref=src, dst_ref=dst, send_sem=ss, recv_sem=rs,
            device_id=dev, device_id_type=MESH,
        )

    sends = []
    guarded = []

    def send_when(there, copies):
        @pl.when(there)
        def _():
            for copy in copies:
                copy.start()

        guarded.append((there, copies))


    def send(src, dst, ss, rs, dev):
        copy = remote(src, dst, ss, rs, dev)
        copy.start()
        sends.append(copy)
        return copy

    barrier = pltpu.get_barrier_semaphore()
    peers = [fdev(zp(k), y) for k in range(1, nz)]
    peers += [fdev(z, yp(j)) for j in range(1, ny)]
    peers += [{"ep": lax.rem(e + i, ne)} for i in range(1, ne)]
    for dev in peers:
        pl.semaphore_signal(barrier, inc=1, device_id=dev, device_id_type=MESH)
    locals_ = []
    for i, (src, dst) in enumerate((
        (up_in.at[0], rows(up, f, up_in.shape[1])),
        (down_in.at[0], rows(down, f, down_in.shape[1])),
        (tok_in, rows(tok, e, T)),
        (cot_in, rows(cot, e, T)),
    )):
        copy = pltpu.make_async_copy(src, dst, local_sem.at[i])
        copy.start()
        locals_.append(copy)
    rows(gate, e, T)[...] = gate_in[e]
    pl.semaphore_wait(barrier, len(peers))

    weights = ((up_in, up), (down_in, down))

    def span(ref, index, size, begin, count):
        return ref.at[pl.ds(pl.multiple_of(index * size + begin, 16), count)]

    def chain(w, sgn, b, src=None):
        full = weights[w][1]
        size = weights[w][0].shape[1]
        block = rows(full, b * ny + y, size)
        way = (1 - sgn) // 2
        return remote(block if src is None else src, block, wz_s.at[w, way, b],
                      wz_r.at[w, way, b], fdev(zp(sgn), y))

    def chain_tail(w, sgn, b, j):
        full = weights[w][1]
        size = weights[w][0].shape[1]
        q = tail_rows(size)
        block = span(full, b * ny + yp(-j), size, size - q, q)
        way = (1 - sgn) // 2
        return remote(block, block, wt_s.at[w, way, b, j - 1], wt_r.at[w, way, b, j - 1],
                      fdev(zp(sgn), y))

    def across(w, b, yy, j):
        full = weights[w][1]
        size = weights[w][0].shape[1]
        block = span(full, b * ny + yy, size, 0, size - tail_rows(size))
        return remote(block, block, wy_s.at[w, b, j - 1], wy_r.at[w, b, j - 1], fdev(z, yp(j)))

    def own_across(w, yy, j, src=None):
        full = weights[w][1]
        size = weights[w][0].shape[1]
        block = rows(full, z * ny + yy, size)
        return remote(block if src is None else src, block, wo_s.at[w, j - 1], wo_r.at[w, j - 1],
                      fdev(z, yp(j)))

    def weight_start(w):
        src = weights[w][0].at[0]
        for sgn in (1, -1):
            send_when(inside(z + sgn), [chain(w, sgn, z, src)])
        for j in range(1, ny):
            copy = own_across(w, y, j, src)
            copy.start()
            sends.append(copy)

    def tail_start(w):
        for j in range(1, ny):
            own_across(w, yp(-j), j).wait_recv()
        for sgn in (1, -1):
            send_when(inside(z + sgn), [chain_tail(w, sgn, z, j) for j in range(1, ny)])

    def hop(w, s):
        for sgn in (1, -1):
            b = zp(-sgn * s)
            there = inside(z - sgn * s)

            @pl.when(there)
            def _():
                chain(w, sgn, b).wait_recv()

            send_when(there & inside(z + sgn), [chain(w, sgn, b)])
            send_when(there, [across(w, b, y, j) for j in range(1, ny)])

    def hop_tail(w, s):
        for sgn in (1, -1):
            b = zp(-sgn * s)
            there = inside(z - sgn * s)

            @pl.when(there)
            def _():
                for j in range(1, ny):
                    chain_tail(w, sgn, b, j).wait_recv()

            send_when(there & inside(z + sgn), [chain_tail(w, sgn, b, j) for j in range(1, ny)])

    def weight_wait(w):
        locals_[w].wait()
        for k in range(1, nz):
            for j in range(1, ny):
                across(w, zp(k), yp(-j), j).wait_recv()

    acts = ((tok_in, tok), (cot_in, cot))

    def act_start(w):
        src, full = acts[w]
        for k in range(1, nx):
            send(src, rows(full, e, T), tx_s.at[w, k - 1], tx_r.at[w, k - 1], edev(xp(k), c))
        send(src, rows(full, e, T), tc_s.at[w, 0], tc_r.at[w, 0], edev(x, 1 - c))

    def act_forward(w):
        src, full = acts[w]
        started = []
        for k in range(1, nx):
            block = rows(full, xp(-k) * 2 + c, T)
            remote(block, block, tx_s.at[w, k - 1], tx_r.at[w, k - 1],
                   edev(xp(k), c)).wait_recv()
            copy = remote(block, block, tc_s.at[w, k], tc_r.at[w, k], edev(x, 1 - c))
            copy.start()
            started.append(copy)
        return started

    def act_wait(w):
        src, full = acts[w]
        locals_[2 + w].wait()
        for k in range(nx):
            block = rows(full, xp(-k) * 2 + 1 - c, T)
            remote(block, block, tc_s.at[w, k], tc_r.at[w, k], edev(x, 1 - c)).wait_recv()

    weight_start(0)
    act_start(0)
    for i in range(1, ne):
        other = lax.rem(e + i, ne)
        send(gate_in.at[other], rows(gate, e, T), g_s.at[i - 1], g_r.at[i - 1], {"ep": other})
    act_start(1)
    hop(0, 1)
    tok_forwards = act_forward(0)
    tail_start(0)
    hop(0, 2)
    hop_tail(0, 1)
    hop(0, 3)
    weight_start(1)
    hop_tail(0, 2)
    hop_tail(0, 3)
    cot_forwards = act_forward(1)

    act_wait(1)
    for copy in cot_forwards:
        copy.wait_send()
    for i in range(1, ne):
        block = rows(gate, lax.rem(e - i + ne, ne), T)
        remote(block, block, g_s.at[i - 1], g_r.at[i - 1], {"ep": lax.rem(e + i, ne)}).wait_recv()

    @tiles(R, 16)
    def _(r):
        cot[r, :] = (cot[r, :].astype(F32) * gate[r, 0:1]).astype(BF16)

    act_wait(0)
    hop(1, 1)
    tail_start(1)
    weight_wait(0)

    @tiles(FF, 256)
    def _(n):
        slope[:, n] = dot(tok[...], up[:, n], NN)

    hop(1, 2)
    hop_tail(1, 1)

    @tiles(R, 16)
    def _(r):
        value, grad = gelu_parts(slope[r, :])
        hidden[r, :] = value.astype(BF16)
        slope[r, :] = grad

    @tiles(D, 512)
    def _(n):
        dpart[:, n] = dot(hidden[...], cot[:, n], TN).astype(BF16)

    parts = ((upart, ry_u, rz_u, rt_u, ft_u, ug_out), (dpart, ry_d, rz_d, rt_d, ft_d, dg_out))

    flip = lax.div(z, 2)
    near = z + flip * (3 - 2 * z)
    order = [d + flip * (3 - 2 * d) for d in (near * 0 + 3, 2 - 2 * near, 1 + near, near)]

    def give(w, d, yy, j):
        part, ry = parts[w][:2]
        size = parts[w][-1].shape[1]
        return remote(span(part, d * ny + yy, size, 0, size - tail_rows(size)),
                      ry.at[(j - 1) * nz + d], ry_s.at[w, d, j - 1], ry_r.at[w, d, j - 1],
                      fdev(z, yp(j)))

    def run_block(w, way, d, nxt):
        part, ry, rz = parts[w][:3]
        size = parts[w][-1].shape[1]
        return remote(rows(part, d * ny + y, size), rz.at[way, d], rz_s.at[w, d],
                      rz_r.at[w, way, d], fdev(nxt, y))

    def run_tail(w, way, d, nxt, j):
        part, rt = parts[w][0], parts[w][3]
        size = parts[w][-1].shape[1]
        q = tail_rows(size)
        return remote(span(part, d * ny + yp(j), size, size - q, q), rt.at[way, d, j - 1],
                      rt_s.at[w, d, j - 1], rt_r.at[w, way, d, j - 1], fdev(nxt, y))

    def last_tail(w, j):
        part, ft = parts[w][0], parts[w][4]
        size = parts[w][-1].shape[1]
        q = tail_rows(size)
        return remote(span(part, z * ny + yp(j), size, size - q, q), ft.at[j - 1],
                      ft_s.at[w, j - 1], ft_r.at[w, j - 1], fdev(z, yp(j)))

    def part_start(w):
        for d in order:
            for j in range(1, ny):
                copy = give(w, d, yp(j), j)
                copy.start()
                sends.append(copy)

    def add(part, start, count, others):
        @tiles(count, 16)
        def _(r):
            at = pl.ds(pl.multiple_of(start + r.start, 16), 16)
            total = part[at, :].astype(F32)
            for other in others:
                total += other[r, :].astype(F32)
            part[at, :] = total.astype(BF16)

    def pair(w, d):
        part, ry = parts[w][:2]
        size = parts[w][-1].shape[1]
        for j in range(1, ny):
            give(w, d, y, j).wait_recv()
        add(part, (d * ny + y) * size, size - tail_rows(size),
            [ry.at[(j - 1) * nz + d] for j in range(1, ny)])

    def run(w, p):
        part, ry, rz, rt = parts[w][:4]
        size = parts[w][-1].shape[1]
        q = tail_rows(size)
        d = order[p]
        way = jnp.where(d > z, 0, 1)
        sgn = 1 - 2 * way
        nxt = z + sgn
        pair(w, d)

        @pl.when(inside(z - sgn))
        def _():
            run_block(w, way, d, nxt).wait_recv()
            for j in range(1, ny):
                run_tail(w, way, d, nxt, j).wait_recv()
            add(part, (d * ny + y) * size, size, [rz.at[way, d]])
            for j in range(1, ny):
                add(part, (d * ny + yp(j)) * size + size - q, q, [rt.at[way, d, j - 1]])

        copies = [run_block(w, way, d, nxt)]
        copies += [run_tail(w, way, d, nxt, j) for j in range(1, ny)]
        for copy in copies:
            copy.start()
            sends.append(copy)

    def part_last(w):
        part, ry, rz, rt = parts[w][:4]
        size = parts[w][-1].shape[1]
        q = tail_rows(size)
        pair(w, z)
        for way in range(2):
            sgn = 1 - 2 * way

            @pl.when(inside(z - sgn))
            def _():
                for j in range(1, ny):
                    run_tail(w, way, z, zp(1), j).wait_recv()
                    add(part, (z * ny + yp(j)) * size + size - q, q, [rt.at[way, z, j - 1]])

        for j in range(1, ny):
            copy = last_tail(w, j)
            copy.start()
            sends.append(copy)
        for way in range(2):
            sgn = 1 - 2 * way

            @pl.when(inside(z - sgn))
            def _():
                run_block(w, way, z, zp(1)).wait_recv()
                add(part, (z * ny + y) * size, size, [rz.at[way, z]])

    def part_end(w):
        part, ry, rz, rt, ft, out = parts[w]
        size = out.shape[1]
        q = tail_rows(size)
        for j in range(1, ny):
            last_tail(w, j).wait_recv()
        add(part, (z * ny + y) * size + size - q, q, [ft.at[j - 1] for j in range(1, ny)])

        @tiles(size, 16)
        def _(r):
            out[0, r, :] = part[pl.ds(pl.multiple_of(f * size + r.start, 16), 16), :]

    backs = ((cot, rc_m, rx_m, mixed_out), (tok, rc_t, rx_t, tg_out))

    def back_start(w):
        full, rc, rx, out = backs[w]
        for k in range(nx):
            k = (k + 1) % nx
            send(rows(full, xp(k) * 2 + 1 - c, T), rc.at[k], rc_s.at[w, k], rc_r.at[w, k],
                 edev(x, 1 - c))

    def back_pair(w):
        full, rc, rx, out = backs[w]
        for k in range(nx):
            k = (k + 1) % nx
            index = xp(k) * 2 + c
            slot = rc.at[k]
            remote(slot, slot, rc_s.at[w, k], rc_r.at[w, k], edev(x, 1 - c)).wait_recv()

            @tiles(T, 16)
            def _(r):
                at = pl.ds(pl.multiple_of(index * T + r.start, 16), 16)
                full[at, :] = (full[at, :].astype(F32) + rc[k, r, :].astype(F32)).astype(BF16)

            if k:
                send(rows(full, index, T), rx.at[k - 1], rx_s.at[w, k - 1], rx_r.at[w, k - 1],
                     edev(xp(k), c))

    def back_end(w):
        full, rc, rx, out = backs[w]
        for k in range(1, nx):
            slot = rx.at[k - 1]
            remote(slot, slot, rx_s.at[w, k - 1], rx_r.at[w, k - 1], edev(xp(k), c)).wait_recv()

        @tiles(T, 16)
        def _(r):
            at = pl.ds(pl.multiple_of(e * T + r.start, 16), 16)
            total = full[at, :].astype(F32)
            for k in range(1, nx):
                total += rx[k - 1, r, :].astype(F32)
            out[r, :] = total.astype(BF16)

    hop(1, 3)
    hop_tail(1, 2)
    part_start(1)
    hop_tail(1, 3)
    weight_wait(1)

    @tiles(FF, 256)
    def _(n):
        dpre[:, n] = (dot(cot[...], down[n, :], NT) * slope[:, n]).astype(BF16)

    run(1, 0)

    @tiles(D, 384)
    def _(n):
        upart[n, :] = dot(tok[:, n], dpre[...], TN).astype(BF16)

    part_start(0)
    run(1, 1)

    @tiles(D, 512)
    def _(n):
        cot[:, n] = (dot(hidden[...], down[:, n], NN) * gate[:, 0:1]).astype(BF16)

    back_start(0)
    run(1, 2)
    for copy in tok_forwards:
        copy.wait_send()

    @tiles(D, 512)
    def _(n):
        tok[:, n] = dot(dpre[...], up[n, :], NT).astype(BF16)

    back_start(1)
    back_pair(0)
    back_pair(1)
    run(0, 0)
    part_last(1)
    back_end(0)
    run(0, 1)
    back_end(1)
    part_end(1)
    run(0, 2)
    part_last(0)
    part_end(0)
    for copy in sends:
        copy.wait_send()
    for there, copies in guarded:
        @pl.when(there)
        def _():
            for copy in copies:
                copy.wait_send()


def body(tokens, expert_ids, gates, up_weight, down_weight, cotangent):
    nf, ne = lax.axis_size("fsdp"), lax.axis_size("ep")
    nz = 4
    ny, nx = nf // nz, ne // 2
    T, D = tokens.shape
    R = ne * T
    su, FF = up_weight.shape[1:]
    sd = down_weight.shape[1]
    chosen = expert_ids[None] == jnp.arange(ne, dtype=jnp.int32)[:, None, None]
    dense = jnp.sum(jnp.where(chosen, gates[None], 0.0), axis=2)
    gcols = jnp.broadcast_to(dense[:, :, None], (ne, T, LANES))
    qu, qd = (tail_rows(size) for size in (su, sd))
    anyspace = pl.BlockSpec(memory_space=pl.ANY)
    vmem = pl.BlockSpec(memory_space=pltpu.VMEM)
    sem = pltpu.SemaphoreType.DMA
    V = pltpu.VMEM
    scratch = [
        V((D, FF), BF16), V((FF, D), BF16), V((R, D), BF16), V((R, D), BF16),
        V((R, LANES), F32), V((R, FF), F32), V((R, FF), BF16), V((R, FF), BF16),
        V((D, FF), BF16), V((FF, D), BF16),
        V(((ny - 1) * nz, su - qu, FF), BF16), V(((ny - 1) * nz, sd - qd, D), BF16),
        V((2, nz, su, FF), BF16), V((2, nz, sd, D), BF16),
        V((2, nz, ny - 1, qu, FF), BF16), V((2, nz, ny - 1, qd, D), BF16),
        V((ny - 1, qu, FF), BF16), V((ny - 1, qd, D), BF16),
        V((nx, T, D), BF16), V((nx, T, D), BF16),
        V((nx - 1, T, D), BF16), V((nx - 1, T, D), BF16),
        sem((4,)),
        sem((2, 2, nz)), sem((2, 2, nz)),
        sem((2, 2, nz, ny - 1)), sem((2, 2, nz, ny - 1)),
        sem((2, ny - 1)), sem((2, ny - 1)),
        sem((2, nz, ny - 1)), sem((2, nz, ny - 1)),
        sem((2, nx - 1)), sem((2, nx - 1)),
        sem((2, nx)), sem((2, nx)),
        sem((ne - 1,)), sem((ne - 1,)),
        sem((2, nz, ny - 1)), sem((2, nz, ny - 1)),
        sem((2, nz)), sem((2, 2, nz)),
        sem((2, nz, ny - 1)), sem((2, 2, nz, ny - 1)),
        sem((2, ny - 1)), sem((2, ny - 1)),
        sem((2, nx)), sem((2, nx)),
        sem((2, nx - 1)), sem((2, nx - 1)),
    ]
    return pl.pallas_call(
        functools.partial(kernel, nz, ny, nx),
        out_shape=(
            jax.ShapeDtypeStruct((T, D), BF16),
            jax.ShapeDtypeStruct((T, D), BF16),
            jax.ShapeDtypeStruct((1, su, FF), BF16),
            jax.ShapeDtypeStruct((1, sd, D), BF16),
        ),
        in_specs=[anyspace, anyspace, vmem, anyspace, anyspace],
        out_specs=(vmem, vmem, vmem, vmem),
        scratch_shapes=scratch,
        compiler_params=pltpu.CompilerParams(
            collective_id=0, has_side_effects=True, vmem_limit_bytes=64 * 1024 * 1024 - 262144
        ),
    )(tokens, cotangent, gcols, up_weight, down_weight)


def solution(mesh):
    placed = (
        P(("fsdp", "ep"), None),
        P(("fsdp", "ep"), None),
        P(("fsdp", "ep"), None),
        P("ep", "fsdp", None),
        P("ep", "fsdp", None),
        P(("fsdp", "ep"), None),
    )
    return jax.shard_map(
        body,
        mesh=mesh,
        in_specs=placed,
        out_specs=(
            P(("fsdp", "ep"), None),
            P(("fsdp", "ep"), None),
            P("ep", "fsdp", None),
            P("ep", "fsdp", None),
        ),
        check_vma=False,
    )
```
